128 devices in a mesh: seq: 32 (over x, y, core), head: 4 (over z).
Axes of the slice: x: 4, y: 4, z: 4, core: 2. Of those that a mesh axis runs over, the one named last changes fastest.
Arguments:
- inputs: float32 [16384, 4096], P('seq', 'head'), may hold values from -6 to 6
- step_raw: float32 [64, 16384], P('head', 'seq'), may hold values from -4 to -2, as said below
- decay_rate: float32 [64], P('head'), may hold values from 0 to 1, as said below
- b_proj: float32 [16384, 128], P('seq'), may hold values from -0.5 to 0.5
- c_proj: float32 [16384, 128], P('seq'), may hold values from -0.5 to 0.5
- grad_out: float32 [16384, 4096], P('seq', 'head'), may hold values from -1.5 to 1.5
Outputs:
- grad_inputs: float32 [16384, 4096], P('seq', 'head')
- grad_step: float32 [64, 16384], P('head', 'seq')
- grad_b: float32 [16384, 128], P('seq')
- grad_c: float32 [16384, 128], P('seq')
The draws below stay inside these ranges and needn't reach their ends.
Inputs may be any that keep to these rules, and one draw needn't show every extreme that they name: `step_raw`: softplus of each entry lies within 0.02 to 0.1. `decay_rate`: positive.
All inputs are finite; a program needn't handle non-finite values.
Results may differ from the reference program's by a relative error of at most 0.00022.
Values sent between devices are 32-bit elements; how exact they have to be, the bound alone decides.
A program may use at most 128 MiB of HBM per device.

```python
import jax
import jax.numpy as jnp
from jax import lax

HEADS = 64
HEAD_DIM = 64
STATE = 128
GROUP = 128
TOKENS = 16384


def draw_step_raw(key, part):
    step_size = jnp.exp(jax.random.uniform(key, (HEADS, TOKENS), jnp.float32, jnp.log(0.02), jnp.log(0.1)))
    return jnp.log(jnp.expm1(step_size))


def draw_decay_rate(key, part):
    first, second, third = jax.random.split(key, 3)
    share = 0.5
    quick = jax.random.uniform(first, (HEADS,), jnp.float32) < share
    slow_rate = jnp.exp(jax.random.uniform(second, (HEADS,), jnp.float32, jnp.log(0.2), 0.0)) * (46.0 / TOKENS)
    quick_rate = jax.random.uniform(third, (HEADS,), jnp.float32, 0.35, 0.7)
    return jnp.where(quick, quick_rate, slow_rate)


def levels(own_key, shape, cuts, smallest, largest):
    loudness = 1.0
    for dim, blocks in cuts:
        heights = jax.random.uniform(jax.random.fold_in(jax.random.fold_in(own_key, 6), dim), (blocks,), jnp.float32, smallest / len(cuts), largest / len(cuts))
        loudness = loudness * jnp.repeat(jnp.exp(heights), shape[dim] // blocks).reshape((-1,) + (1,) * (len(shape) - 1 - dim))
    return loudness


def bell_draw(rng, dims, width, limit, shards=(), kind=jnp.bfloat16):
    array = width * jax.random.normal(rng, dims, jnp.float32)
    if shards:
        array = array * levels(rng, dims, shards, -0.22, 0.18)
    return jnp.clip(array, -limit, limit).astype(kind)


def setup_inputs(seed: int = 0) -> dict:
    keys = jax.random.split(jax.random.key(seed), 7)
    return {
        "inputs": bell_draw(keys[0], (TOKENS, HEADS * HEAD_DIM), 1.0, 6.0, ((0, 32), (1, 4)), jnp.float32),
        "step_raw": draw_step_raw(jax.random.fold_in(keys[6], 71), 0),
        "decay_rate": draw_decay_rate(jax.random.fold_in(keys[6], 71), 0),
        "b_proj": bell_draw(keys[3], (TOKENS, STATE), STATE ** -0.5, 0.5, ((0, 32),), jnp.float32),
        "c_proj": bell_draw(keys[4], (TOKENS, STATE), STATE ** -0.5, 0.5, ((0, 32),), jnp.float32),
        "grad_out": bell_draw(keys[5], (TOKENS, HEADS * HEAD_DIM), 0.25, 1.5, ((0, 32), (1, 4)), jnp.float32),
    }


precise = lax.Precision.HIGHEST

def group_parts(inputs_heads, step_size, decay_rate, b_proj):
    length = inputs_heads.shape[0]
    heads = inputs_heads.shape[1]
    blocks = length // GROUP
    log_decay = -decay_rate[:, None] * step_size
    cumulative = jnp.cumsum(log_decay.reshape(heads, blocks, GROUP), axis=2)
    x_blocks = inputs_heads.reshape(blocks, GROUP, heads, HEAD_DIM)
    b_blocks = b_proj.reshape(blocks, GROUP, STATE)
    step_blocks = step_size.reshape(heads, blocks, GROUP)
    to_end = jnp.exp(cumulative[:, :, -1:] - cumulative) * step_blocks
    contrib = jnp.einsum('hcj,cjn,cjhp->chnp', to_end, b_blocks, x_blocks, precision=precise)
    block_decay = jnp.exp(cumulative[:, :, -1])
    return (cumulative, step_blocks, x_blocks, b_blocks, contrib, block_decay)

def advance(carried, element):
    factor, added = element
    return (factor[:, None, None] * carried + added, carried)

def direction(inputs_heads, step_size, decay_rate, b_proj, c_proj, initial):
    cumulative, step_blocks, x_blocks, b_blocks, contrib, block_decay = group_parts(inputs_heads, step_size, decay_rate, b_proj)
    blocks = x_blocks.shape[0]
    c_blocks = c_proj.reshape(blocks, GROUP, STATE)
    gram = jnp.einsum('cin,cjn->cij', c_blocks, b_blocks, precision=precise)
    lower = jnp.arange(GROUP)[:, None] >= jnp.arange(GROUP)[None, :]
    spread = cumulative[:, :, :, None] - cumulative[:, :, None, :]
    weights = gram[None] * jnp.exp(jnp.where(lower, spread, -jnp.inf)) * step_blocks[:, :, None, :]
    inner = jnp.einsum('hcij,cjhp->cihp', weights, x_blocks, precision=precise)
    final, before = lax.scan(advance, initial, (block_decay.T, contrib))
    outer = jnp.einsum('cin,chnp,hci->cihp', c_blocks, before, jnp.exp(cumulative), precision=precise)
    combined = inner + outer
    return (combined.reshape(blocks * GROUP, -1), final)

def two_ways(inputs_heads, step_raw, decay_rate, b_proj, c_proj, from_left, from_right):
    step_size = jax.nn.softplus(step_raw)
    forward_out, forward_last = direction(inputs_heads, step_size, decay_rate, b_proj, c_proj, from_left)
    backward_out, backward_last = direction(inputs_heads[::-1], step_size[:, ::-1], decay_rate, b_proj[::-1], c_proj[::-1], from_right)
    return (forward_out + backward_out[::-1], forward_last, backward_last)

def reference(inputs, step_raw, decay_rate, b_proj, c_proj, grad_out):
    length = inputs.shape[0]
    per_head = inputs.reshape(length, HEADS, HEAD_DIM).transpose(1, 0, 2)
    cot_heads = grad_out.reshape(length, HEADS, HEAD_DIM).transpose(1, 0, 2)
    empty = jnp.zeros((1, STATE, HEAD_DIM), jnp.float32)

    def one_head(sums, element):
        x_head, raw_head, rate_head, cot_head = element

        def mapped(x_part, raw_part, b_part, c_part):
            return two_ways(x_part[:, None, :], raw_part[None, :], rate_head[None], b_part, c_part, empty, empty)[0]
        _, pull = jax.vjp(mapped, x_head, raw_head, b_proj, c_proj)
        grad_x, grad_raw, grad_bpart, grad_cpart = pull(cot_head)
        return ((sums[0] + grad_bpart, sums[1] + grad_cpart), (grad_x, grad_raw))
    start = (jnp.zeros((length, STATE), jnp.float32), jnp.zeros((length, STATE), jnp.float32))
    sums, stacked = lax.scan(one_head, start, (per_head, step_raw, decay_rate, cot_heads))
    grad_inputs = stacked[0].transpose(1, 0, 2).reshape(length, HEADS * HEAD_DIM)
    return (grad_inputs, stacked[1], sums[0], sums[1])
```

```python
import jax
import jax.numpy as jnp
from jax import lax
from jax.experimental import pallas as pl
from jax.experimental.pallas import tpu as pltpu
from jax.sharding import PartitionSpec as P

HEAD_DIM = 64
STATE = 128
CHIPS = 16
TILE = 256
F32 = jnp.float32
BF16 = jnp.bfloat16
MESH = pl.DeviceIdType.MESH


def split2(a):
    high = a.astype(BF16)
    return high, (a - high.astype(F32)).astype(BF16)


def split3(a):
    first = a.astype(BF16)
    rest = a - first.astype(F32)
    second = rest.astype(BF16)
    return first, second, (rest - second.astype(F32)).astype(BF16)


def nn(a, b):
    return lax.dot_general(a, b, (((1,), (0,)), ((), ())), preferred_element_type=F32)


def nt(a, b):
    return lax.dot_general(a, b, (((1,), (1,)), ((), ())), preferred_element_type=F32)


def nn3(a, b):
    return nn(a[0], b[0]) + (nn(a[0], b[1]) + nn(a[1], b[0]))


def nt3(a, b):
    return nt(a[0], b[0]) + (nt(a[0], b[1]) + nt(a[1], b[0]))


def iota(shape, axis):
    return lax.broadcasted_iota(jnp.int32, shape, axis)


def kernel(
    x_ref, g_ref, raw_ref, rate_ref, b_ref, c_ref,
    gx_ref, graw_ref, gb_ref, gc_ref,
    ft, fac, xg, bt, ct, bs, cs, gm, amat, inner,
    v, dec, pv, pdec, vc, dc, r1, dr, r2, r3, ein, eout, es, edge,
    acc, z1, acc2, z2, red,
    pair_send, pair_recv, out_send, out_recv, dec_send, dec_recv,
    back_send, back_recv, z_send, z_recv,
):
    seq = lax.axis_index("seq")
    zed = lax.axis_index("head")
    chip = seq // 2
    core = seq % 2
    other = 1 - core
    partner = (2 * chip + other, zed)
    z_even = zed + 1 - 2 * (zed % 2)
    z_odd = (zed + 1 + 2 * ((zed + 1) % 2)) % 4
    length = x_ref.shape[0]
    heads = raw_ref.shape[0]
    half = length // 2
    first = (core == 0).astype(F32)
    second = 1.0 - first

    def peer(offset):
        return (chip + offset) % CHIPS

    barrier = pltpu.get_barrier_semaphore()
    for offset in range(1, CHIPS):
        pl.semaphore_signal(barrier, inc=1, device_id=(2 * peer(offset) + core, zed), device_id_type=MESH)
    for target in (partner, (seq, z_even), (seq, z_odd)):
        pl.semaphore_signal(barrier, inc=1, device_id=target, device_id_type=MESH)

    def lanes(tile):
        return pl.ds(pl.multiple_of(tile * TILE, TILE), TILE)

    raw = raw_ref[...]
    step = jnp.maximum(raw, 0.0) + jnp.log1p(jnp.exp(-jnp.abs(raw)))
    rate = rate_ref[...]
    log_decay = -rate * step
    rows = iota((length, length), 0)
    cols = iota((length, length), 1)
    upto = (rows <= cols).astype(F32).astype(BF16)
    sums = nn(jnp.concatenate(split3(log_decay), axis=0), upto)
    run = sums[:heads] + (sums[heads : 2 * heads] + sums[2 * heads :])
    before = run - log_decay
    factors = jnp.concatenate(
        [step * jnp.exp(-run), step * jnp.exp(before), jnp.exp(run), jnp.exp(-before)], axis=0
    )
    parts = [p.astype(F32) for p in split3(factors)]
    stack = jnp.concatenate(parts + [jnp.zeros_like(factors)], axis=0)
    ft[...] = jnp.transpose(stack).astype(BF16)
    for src, flat, turned in ((b_ref, bs, bt), (c_ref, cs, ct)):
        full = src[...]
        flat[0], flat[1] = split2(full)
        turned[0], turned[1] = split2(jnp.transpose(full))

    def pair(ref, *index):
        return ref[(0,) + index], ref[(1,) + index]

    def summarise(tile, block, offset):
        spread = ft[...]
        r = iota((TILE, TILE), 0)
        col = iota((TILE, TILE), 1)
        out = []
        for q in range(4):
            hot = ((r % 64) == q * 16 + tile * 4 + col // HEAD_DIM) & (r < 192)
            factor = nn(spread, hot.astype(F32).astype(BF16))
            fac[q, :, lanes(tile)] = factor
            source = x_ref if q < 2 else g_ref
            scaled = split2(factor * source[:, lanes(tile)])
            xg[q, 0, :, lanes(tile)] = scaled[0]
            xg[q, 1, :, lanes(tile)] = scaled[1]
            left = bt if q < 2 else ct
            out.append(nn3((left[0], left[1]), scaled))
            if q == 2:
                whole = factor[length - 1 : length, :]
        for flow, value in ((0, out[0] * whole), (1, out[3] * whole), (2, out[1]), (3, out[2])):
            v[block, :, flow, :, offset : offset + TILE] = value.reshape(CHIPS, 8, TILE)
        dec[block, :, offset : offset + TILE] = whole

    for j in range(2):
        summarise(2 * other + j, other, j * TILE)
    pl.semaphore_wait(barrier, CHIPS + 2)
    to_partner = [
        pltpu.make_async_remote_copy(v.at[other], pv, pair_send.at[0], pair_recv.at[0], device_id=partner, device_id_type=MESH),
        pltpu.make_async_remote_copy(dec.at[other], pdec, pair_send.at[1], pair_recv.at[1], device_id=partner, device_id_type=MESH),
    ]
    for copy in to_partner:
        copy.start()
    for j in range(2):
        summarise(2 * core + j, core, j * TILE)
    for copy in to_partner:
        copy.wait()

    own_decay = dec[core]
    mate_decay = pdec[...]
    ahead_own = first * mate_decay + second
    ahead_mate = first + second * own_decay
    behind_own = first + second * mate_decay
    behind_mate = first * own_decay + second
    dc[0] = own_decay * mate_decay

    def join(index):
        for flow in range(4):
            a, b = (ahead_own, ahead_mate) if flow < 2 else (behind_own, behind_mate)
            vc[index, flow] = a * v[core, index, flow] + b * pv[index, flow]

    outgoing = []
    for offset in range(1, CHIPS):
        there = peer(offset)
        join(there)
        device = (2 * there + core, zed)
        copy = pltpu.make_async_remote_copy(vc.at[there], r1.at[chip], out_send.at[offset], out_recv.at[offset], device_id=device, device_id_type=MESH)
        copy.start()
        outgoing.append(copy)
        copy = pltpu.make_async_remote_copy(dc.at[0], dr.at[chip], dec_send.at[offset], dec_recv.at[offset], device_id=device, device_id_type=MESH)
        copy.start()
        outgoing.append(copy)
    join(chip)
    r1[chip] = vc[chip]
    dr[chip] = dc[0]

    for r in range(2):
        row = slice(r * half, (r + 1) * half)
        forward = nt3((cs[0, row], cs[1, row]), (bs[0], bs[1]))
        backward = nt3((bs[0, row], bs[1, row]), (cs[0], cs[1]))
        i = iota((half, length), 0) + r * half
        j = iota((half, length), 1)
        for m, (value, keep) in enumerate(((forward, i >= j), (forward, i <= j), (backward, i <= j), (backward, i >= j))):
            gm[m, 0, row], gm[m, 1, row] = split2(jnp.where(keep, value, 0.0))

    def masked(m, source, tile, slot):
        lower = m % 2 == 0 if m < 2 else m == 3
        for r in range(2):
            row = slice(r * half, (r + 1) * half)
            if lower:
                depth = slice(0, (r + 1) * half)
            else:
                depth = slice(r * half, length)
            left = (gm[m, 0, row, depth], gm[m, 1, row, depth])
            right = (xg[source, 0, depth, lanes(tile)], xg[source, 1, depth, lanes(tile)])
            inner[slot, row, lanes(tile)] = nn3(left, right)

    def input_side(tile, carry):
        masked(2, 2, tile, 2)
        masked(3, 3, tile, 3)
        return carry

    lax.fori_loop(0, 4, input_side, 0)

    for copy in outgoing:
        copy.wait()
    ahead = [jnp.zeros((8, 2 * TILE), F32)] * 2
    for index in range(CHIPS):
        factor = dr[index]
        for flow in range(2):
            r2[index, flow] = ahead[flow]
            ahead[flow] = r1[index, flow] + factor * ahead[flow]
    behind = [jnp.zeros((8, 2 * TILE), F32)] * 2
    for index in reversed(range(CHIPS)):
        factor = dr[index]
        for flow in range(2):
            r2[index, 2 + flow] = behind[flow]
            behind[flow] = r1[index, 2 + flow] + factor * behind[flow]
    returning = []
    for offset in range(1, CHIPS):
        there = peer(offset)
        copy = pltpu.make_async_remote_copy(
            r2.at[there], r3.at[chip], back_send.at[offset], back_recv.at[offset], device_id=(2 * there + core, zed), device_id_type=MESH
        )
        copy.start()
        returning.append(copy)
    r3[chip] = r2[chip]

    amat[...] = jnp.zeros_like(amat)
    low = iota((half, half), 0) >= iota((half, half), 1)
    high = iota((half, half), 0) <= iota((half, half), 1)

    def output_side(tile, carry):
        masked(0, 0, tile, 0)
        masked(1, 1, tile, 1)
        upper = slice(0, half)
        under = slice(half, length)

        def block(a, row, b, col):
            return nt3(pair(xg.at[a], row, lanes(tile)), pair(xg.at[b], col, lanes(tile)))

        for part in (upper, under):
            amat[part, part] += jnp.where(low, block(2, part, 0, part), 0.0) + jnp.where(high, block(3, part, 1, part), 0.0)
        amat[under, upper] += block(2, under, 0, upper)
        amat[upper, under] += block(3, upper, 1, under)
        return carry

    lax.fori_loop(0, 4, output_side, 0)
    whole_a = amat[...]
    from_b = nn3(split2(whole_a), (bs[0], bs[1]))
    from_c = nn3(split2(jnp.transpose(whole_a)), (cs[0], cs[1]))
    for r in range(2):
        acc[r, 0] = from_c[r * half : (r + 1) * half]
        acc[r, 1] = from_b[r * half : (r + 1) * half]

    for copy in returning:
        copy.wait()

    def arrive(index, carry):
        for flow in range(4):
            value = r3[index, flow]
            if flow < 2:
                mine, mate = first, second
            else:
                mine, mate = second, first
            ein[core, index, flow] = (mine + mate * mate_decay) * value + mate * pv[index, flow]
            eout[index, flow] = (mate + mine * own_decay) * value + mine * v[core, index, flow]
        return carry

    lax.fori_loop(0, CHIPS, arrive, 0)
    give = pltpu.make_async_remote_copy(eout, ein.at[core], pair_send.at[2], pair_recv.at[2], device_id=partner, device_id_type=MESH)
    give.start()

    edge[...] = jnp.zeros_like(edge)

    def project(block, offset):
        tile = 2 * block + offset // TILE
        lane = slice(offset, offset + TILE)
        whole = dec[block, :, lane]
        state = [ein[block, :, flow, :, lane].reshape(STATE, TILE) for flow in range(4)]
        local_f = v[block, :, 0, :, lane].reshape(STATE, TILE)
        local_g = v[block, :, 2, :, lane].reshape(STATE, TILE)
        edge[0:1, lanes(tile)] = jnp.sum(state[3] * (local_f + whole * state[0]), axis=0, keepdims=True)
        edge[1:2, lanes(tile)] = jnp.sum(state[1] * (local_g + whole * state[2]), axis=0, keepdims=True)
        scaled = [split2(state[0]), split2(whole * state[2]), split2(whole * state[3]), split2(state[1])]
        for m in range(4):
            es[m, 0, :, lanes(tile)] = scaled[m][0]
            es[m, 1, :, lanes(tile)] = scaled[m][1]
        rows_of = [pair(xg.at[q], slice(None), lanes(tile)) for q in range(4)]
        read = nt3(rows_of[2], scaled[0]) + nt3(rows_of[3], scaled[1])
        write = nt3(rows_of[0], scaled[2]) + nt3(rows_of[1], scaled[3])
        for r in range(2):
            acc[r, 0] += write[r * half : (r + 1) * half]
            acc[r, 1] += read[r * half : (r + 1) * half]

    for j in range(2):
        project(core, j * TILE)
    give.wait()
    for j in range(2):
        project(other, j * TILE)

    def exchange(src, dst, first_sem, targets):
        copies = []
        for r in range(2):
            copies.append(pltpu.make_async_remote_copy(
                src.at[r], dst.at[r], z_send.at[first_sem + r], z_recv.at[first_sem + r], device_id=(seq, targets[r]), device_id_type=MESH
            ))
        for copy in copies:
            copy.start()
        return copies

    copies = exchange(acc, z1, 0, (z_even, z_odd))
    red[...] = jnp.zeros_like(red)

    def finish(tile, carry):
        lane = lanes(tile)
        full = slice(None)
        c_pair = (cs[0], cs[1])
        b_pair = (bs[0], bs[1])
        out_f = inner[0, :, lane] + nn3(c_pair, pair(es.at[0], full, lane))
        out_b = inner[1, :, lane] + nn3(c_pair, pair(es.at[1], full, lane))
        in_f = fac[0, :, lane] * (inner[2, :, lane] + nn3(b_pair, pair(es.at[2], full, lane)))
        in_b = fac[1, :, lane] * (inner[3, :, lane] + nn3(b_pair, pair(es.at[3], full, lane)))
        grad = in_f + in_b
        gx_ref[:, lane] = grad
        x = x_ref[:, lane]
        g = g_ref[:, lane]
        terms = (x * grad, g * (fac[2, :, lane] * out_f) - x * in_f, g * (fac[3, :, lane] * out_b) - x * in_b)
        r = iota((TILE, STATE), 0)
        col = iota((TILE, STATE), 1)
        total = red[...]
        for m in range(3):
            hot = (col == 16 * m + tile * 4 + r // HEAD_DIM).astype(F32).astype(BF16)
            a, b = split2(terms[m])
            total = total + (nn(a, hot) + nn(b, hot))
        red[...] = total
        return carry

    lax.fori_loop(0, 2, finish, 0)
    for copy in copies:
        copy.wait()
    acc2[...] = acc[...] + z1[...]
    copies = exchange(acc2, z2, 2, (z_odd, z_even))
    lax.fori_loop(2, 4, finish, 0)

    turned_red = jnp.transpose(red[...])
    direct = turned_red[:heads]
    hot = (iota((4 * TILE, STATE), 1) == iota((4 * TILE, STATE), 0) // HEAD_DIM).astype(F32).astype(BF16)
    edges = [nn(p, hot) for p in split3(edge[...])]
    edges = jnp.transpose(edges[0] + (edges[1] + edges[2]))
    after = (rows >= cols).astype(F32).astype(BF16)

    def running(value, matrix):
        out = nn(jnp.concatenate(split3(value), axis=0), matrix)
        return out[:heads] + (out[heads : 2 * heads] + out[2 * heads :])

    log_grad = running(turned_red[heads : 2 * heads], after) + edges[:heads, 0:1]
    log_grad = log_grad + running(turned_red[2 * heads : 3 * heads], upto) + edges[:heads, 1:2]
    graw_ref[...] = (direct / step - rate * log_grad) * jax.nn.sigmoid(raw)

    for copy in copies:
        copy.wait()
    for r in range(2):
        row = slice(r * half, (r + 1) * half)
        gb_ref[row] = acc2[r, 0] + z2[r, 0]
        gc_ref[row] = acc2[r, 1] + z2[r, 1]


def on_device(inputs, step_raw, decay_rate, b_proj, c_proj, grad_out):
    length, width = inputs.shape
    heads = step_raw.shape[0]
    vmem = pl.BlockSpec(memory_space=pltpu.VMEM)
    block = (CHIPS, 4, 8, width // 2)
    square = (length, length)
    half = length // 2
    dma = pltpu.SemaphoreType.DMA
    scratch = [
        pltpu.VMEM((length, 256), BF16),
        pltpu.VMEM((4, length, width), F32),
        pltpu.VMEM((4, 2, length, width), BF16),
        pltpu.VMEM((2, STATE, length), BF16),
        pltpu.VMEM((2, STATE, length), BF16),
        pltpu.VMEM((2, length, STATE), BF16),
        pltpu.VMEM((2, length, STATE), BF16),
        pltpu.VMEM((4, 2) + square, BF16),
        pltpu.VMEM(square, F32),
        pltpu.VMEM((4, length, width), F32),
        pltpu.VMEM((2,) + block, F32),
        pltpu.VMEM((2, 1, width // 2), F32),
        pltpu.VMEM(block, F32),
        pltpu.VMEM((1, width // 2), F32),
        pltpu.VMEM(block, F32),
        pltpu.VMEM((1, 1, width // 2), F32),
        pltpu.VMEM(block, F32),
        pltpu.VMEM((CHIPS, 1, width // 2), F32),
        pltpu.VMEM(block, F32),
        pltpu.VMEM(block, F32),
        pltpu.VMEM((2,) + block, F32),
        pltpu.VMEM(block, F32),
        pltpu.VMEM((4, 2, STATE, width), BF16),
        pltpu.VMEM((8, width), F32),
        pltpu.VMEM((2, 2, half, STATE), F32),
        pltpu.VMEM((2, 2, half, STATE), F32),
        pltpu.VMEM((2, 2, half, STATE), F32),
        pltpu.VMEM((2, 2, half, STATE), F32),
        pltpu.VMEM((length, STATE), F32),
        dma((3,)),
        dma((3,)),
        dma((CHIPS,)),
        dma((CHIPS,)),
        dma((CHIPS,)),
        dma((CHIPS,)),
        dma((CHIPS,)),
        dma((CHIPS,)),
        dma((4,)),
        dma((4,)),
    ]
    return pl.pallas_call(
        kernel,
        out_shape=(
            jax.ShapeDtypeStruct((length, width), F32),
            jax.ShapeDtypeStruct((heads, length), F32),
            jax.ShapeDtypeStruct((length, STATE), F32),
            jax.ShapeDtypeStruct((length, STATE), F32),
        ),
        in_specs=[vmem] * 6,
        out_specs=(vmem,) * 4,
        scratch_shapes=scratch,
        compiler_params=pltpu.CompilerParams(
            collective_id=0, has_side_effects=True, vmem_limit_bytes=67043328
        ),
        name="scan_backward",
    )(inputs, grad_out, step_raw, decay_rate.reshape(heads, 1), b_proj, c_proj)


def solution(mesh):
    return jax.shard_map(
        on_device,
        mesh=mesh,
        in_specs=(
            P("seq", "head"),
            P("head", "seq"),
            P("head"),
            P("seq", None),
            P("seq", None),
            P("seq", "head"),
        ),
        out_specs=(P("seq", "head"), P("head", "seq"), P("seq", None), P("seq", None)),
        check_vma=False,
    )
```

```python
import jax
import jax.numpy as jnp
from jax import lax
from jax.experimental import pallas as pl
from jax.experimental.pallas import tpu as pltpu
from jax.sharding import PartitionSpec as P

HEAD_DIM = 64
STATE = 128
CHIPS = 16
TILE = 256
F32 = jnp.float32
BF16 = jnp.bfloat16
MESH = pl.DeviceIdType.MESH


def split2(a):
    high = a.astype(BF16)
    return high, (a - high.astype(F32)).astype(BF16)


def split3(a):
    first = a.astype(BF16)
    rest = a - first.astype(F32)
    second = rest.astype(BF16)
    return first, second, (rest - second.astype(F32)).astype(BF16)


def nn(a, b):
    return lax.dot_general(a, b, (((1,), (0,)), ((), ())), preferred_element_type=F32)


def nt(a, b):
    return lax.dot_general(a, b, (((1,), (1,)), ((), ())), preferred_element_type=F32)


def nn3(a, b):
    return nn(a[0], b[0]) + (nn(a[0], b[1]) + nn(a[1], b[0]))


def nt3(a, b):
    return nt(a[0], b[0]) + (nt(a[0], b[1]) + nt(a[1], b[0]))


def iota(shape, axis):
    return lax.broadcasted_iota(jnp.int32, shape, axis)


OFFSETS = sorted(
    ((dx, dy) for dx in range(4) for dy in range(4) if dx or dy),
    key=lambda o: -(min(o[0], 4 - o[0]) + min(o[1], 4 - o[1])),
)


def kernel(
    x_hbm, g_hbm, raw_hbm, rate_hbm, b_hbm, c_hbm,
    gx_hbm, graw_ref, gb_ref, gc_ref,
    x_ref, g_ref, raw_ref, rate_ref, b_ref, c_ref, gx_ref,
    ft, fac, xg, bt, ct, bs, cs, gm, amat, inner,
    v, dec, pv, pdec, vc, dc, r1, dr, r2, r3, ein, eout, es, edge,
    acc, z1, acc2, z2, red,
    load_sem, store_sem, pair_send, pair_recv, out_send, out_recv, dec_send, dec_recv,
    back_send, back_recv, give_send, give_recv, z_send, z_recv,
):
    seq = lax.axis_index("seq")
    zed = lax.axis_index("head")
    chip = seq // 2
    core = seq % 2
    other = 1 - core
    chip_x = chip // 4
    chip_y = chip % 4
    partner = (2 * chip + other, zed)
    z_even = zed + 1 - 2 * (zed % 2)
    z_odd = (zed + 1 + 2 * ((zed + 1) % 2)) % 4
    length = x_ref.shape[0]
    heads = raw_ref.shape[0]
    half = length // 2
    first = (core == 0).astype(F32)
    second = 1.0 - first

    def peer(offset):
        dx, dy = OFFSETS[offset]
        return ((chip_x + dx) % 4) * 4 + (chip_y + dy) % 4

    def remote(src, dst, send, recv, device):
        return pltpu.make_async_remote_copy(src, dst, send, recv, device_id=device, device_id_type=MESH)

    barrier = pltpu.get_barrier_semaphore()
    for offset in range(CHIPS - 1):
        pl.semaphore_signal(barrier, inc=1, device_id=(2 * peer(offset) + core, zed), device_id_type=MESH)
    for target in (partner, (seq, z_even), (seq, z_odd)):
        pl.semaphore_signal(barrier, inc=1, device_id=target, device_id_type=MESH)
    loads = []
    for n, (src, dst) in enumerate((
        (raw_hbm, raw_ref), (rate_hbm, rate_ref), (c_hbm, c_ref), (g_hbm, g_ref), (b_hbm, b_ref), (x_hbm, x_ref)
    )):
        loads.append(pltpu.make_async_copy(src, dst, load_sem.at[n]))
        loads[-1].start()

    def lanes(tile):
        return pl.ds(pl.multiple_of(tile * TILE, TILE), TILE)

    rows = iota((length, length), 0)
    cols = iota((length, length), 1)
    upto = (rows <= cols).astype(F32).astype(BF16)
    loads[0].wait()
    loads[1].wait()
    raw = raw_ref[...]
    step = jnp.maximum(raw, 0.0) + jnp.log1p(jnp.exp(-jnp.abs(raw)))
    eye = iota((heads, heads), 0) == iota((heads, heads), 1)
    rate = jnp.sum(jnp.where(eye, rate_ref[...], 0.0), axis=1, keepdims=True)
    log_decay = -rate * step
    sums = nn(jnp.concatenate(split3(log_decay), axis=0), upto)
    run = sums[:heads] + (sums[heads : 2 * heads] + sums[2 * heads :])
    before = run - log_decay
    factors = jnp.concatenate(
        [step * jnp.exp(-run), step * jnp.exp(before), jnp.exp(run), jnp.exp(-before)], axis=0
    )
    parts = [p.astype(F32) for p in split3(factors)]
    stack = jnp.concatenate(parts + [jnp.zeros_like(factors)], axis=0)
    ft[...] = jnp.transpose(stack).astype(BF16)

    def turn(src, flat, turned):
        full = src[...]
        flat[0], flat[1] = split2(full)
        turned[0], turned[1] = split2(jnp.transpose(full))

    def pair(ref, *index):
        return ref[(0,) + index], ref[(1,) + index]

    def summarise(batch, tile, block, offset):
        spread = ft[...]
        r = iota((TILE, TILE), 0)
        col = iota((TILE, TILE), 1)
        source = (g_ref if batch == 0 else x_ref)[:, lanes(tile)]
        left = ct if batch == 0 else bt
        lane = slice(offset, offset + TILE)
        for q in ((2, 3) if batch == 0 else (1, 0)):
            hot = ((r % 64) == q * 16 + tile * 4 + col // HEAD_DIM) & (r < 192)
            factor = nn(spread, hot.astype(F32).astype(BF16))
            fac[q, :, lanes(tile)] = factor
            scaled = split2(factor * source)
            xg[q, 0, :, lanes(tile)] = scaled[0]
            xg[q, 1, :, lanes(tile)] = scaled[1]
            value = nn3((left[0], left[1]), scaled)
            if q == 2:
                dec[block, :, lane] = factor[length - 1 : length, :]
            if q in (0, 3):
                value = value * dec[block, :, lane]
            v[batch, block, :, int(q in (0, 3)), :, lane] = value.reshape(CHIPS, 8, TILE)

    def to_partner(batch):
        copies = [remote(v.at[batch, other], pv.at[batch], pair_send.at[batch], pair_recv.at[batch], partner)]
        if batch == 0:
            copies.append(remote(dec.at[other], pdec, pair_send.at[2], pair_recv.at[2], partner))
        for copy in copies:
            copy.start()
        return copies

    def gather(batch):
        own_decay = dec[core]
        mate_decay = pdec[...]
        if batch == 0:
            dc[0] = own_decay * mate_decay
        weights = (
            (first + second * mate_decay, first * own_decay + second),
            (first * mate_decay + second, first + second * own_decay),
        )

        def join(index):
            for flow in range(2):
                a, b = weights[flow]
                vc[batch, index, flow] = a * v[batch, core, index, flow] + b * pv[batch, index, flow]

        copies = []
        for offset in range(CHIPS - 1):
            there = peer(offset)
            join(there)
            device = (2 * there + core, zed)
            n = batch * CHIPS + offset
            copies.append(remote(vc.at[batch, there], r1.at[batch, chip], out_send.at[n], out_recv.at[n], device))
            copies[-1].start()
            if batch == 0:
                copies.append(remote(dc.at[0], dr.at[chip], dec_send.at[offset], dec_recv.at[offset], device))
                copies[-1].start()
        join(chip)
        r1[batch, chip] = vc[batch, chip]
        if batch == 0:
            dr[chip] = dc[0]
        return copies

    def scan_chips(batch, arrived):
        for copy in arrived:
            copy.wait()
        state = jnp.zeros((8, 2 * TILE), F32)
        for index in range(CHIPS):
            r2[batch, index, 1] = state
            state = r1[batch, index, 1] + dr[index] * state
        state = jnp.zeros((8, 2 * TILE), F32)
        for index in reversed(range(CHIPS)):
            r2[batch, index, 0] = state
            state = r1[batch, index, 0] + dr[index] * state
        copies = []
        for offset in range(CHIPS - 1):
            there = peer(offset)
            n = batch * CHIPS + offset
            copies.append(remote(r2.at[batch, there], r3.at[batch, chip], back_send.at[n], back_recv.at[n], (2 * there + core, zed)))
            copies[-1].start()
        r3[batch, chip] = r2[batch, chip]
        return copies

    def arrive(batch, returned):
        for copy in returned:
            copy.wait()
        own_decay = dec[core]
        mate_decay = pdec[...]

        def one(index, carry):
            for flow in range(2):
                mine, mate = (second, first) if flow == 0 else (first, second)
                value = r3[batch, index, flow]
                ein[batch, core, index, flow] = (mine + mate * mate_decay) * value + mate * pv[batch, index, flow]
                eout[batch, index, flow] = (mate + mine * own_decay) * value + mine * v[batch, core, index, flow]
            return carry

        lax.fori_loop(0, CHIPS, one, 0)
        give = remote(eout.at[batch], ein.at[batch, core], give_send.at[batch], give_recv.at[batch], partner)
        give.start()
        return give

    def project(batch, block, offset):
        tile = 2 * block + offset // TILE
        lane = slice(offset, offset + TILE)
        whole = dec[block, :, lane]
        early, late = [ein[batch, block, :, flow, :, lane].reshape(STATE, TILE) for flow in range(2)]
        if batch == 0:
            scaled = ((2, split2(whole * early)), (3, split2(late)))
        else:
            scaled = ((0, split2(late)), (1, split2(whole * early)))
            adjoint_early, adjoint_late = [ein[0, block, :, flow, :, lane].reshape(STATE, TILE) for flow in range(2)]
            local_early, local_late = [v[1, block, :, flow, :, lane].reshape(STATE, TILE) for flow in range(2)]
            edge[0:1, lanes(tile)] = jnp.sum(adjoint_early * (local_late + whole * late), axis=0, keepdims=True)
            edge[1:2, lanes(tile)] = jnp.sum(adjoint_late * (local_early + whole * early), axis=0, keepdims=True)
        total = None
        for m, value in scaled:
            es[m, 0, :, lanes(tile)] = value[0]
            es[m, 1, :, lanes(tile)] = value[1]
            term = nt3(pair(xg.at[(m + 2) % 4], slice(None), lanes(tile)), value)
            total = term if total is None else total + term
        for r in range(2):
            acc[batch, r] += total[r * half : (r + 1) * half]

    def exchange(batch, step_index, src, dst, targets):
        copies = []
        for r in range(2):
            n = 4 * batch + 2 * step_index + r
            copies.append(remote(src.at[batch, r], dst.at[batch, r], z_send.at[n], z_recv.at[n], (seq, targets[r])))
            copies[-1].start()
        return copies

    def exchange_again(batch, copies):
        for copy in copies:
            copy.wait()
        acc2[batch] = acc[batch] + z1[batch]
        return exchange(batch, 1, acc2, z2, (z_odd, z_even))

    def exchange_end(batch, copies, out):
        for copy in copies:
            copy.wait()
        for r in range(2):
            out[r * half : (r + 1) * half] = acc2[batch, r] + z2[batch, r]

    def add_heads(tile, terms):
        r = iota((TILE, STATE), 0)
        col = iota((TILE, STATE), 1)
        total = red[...]
        for m, term in terms:
            hot = (col == 16 * m + tile * 4 + r // HEAD_DIM).astype(F32).astype(BF16)
            a, b = split2(term)
            total = total + (nn(a, hot) + nn(b, hot))
        red[...] = total

    def finish_inputs(tile, carry):
        lane = lanes(tile)
        full = slice(None)
        b_pair = (bs[0], bs[1])
        in_f = fac[0, :, lane] * (inner[2, :, lane] + nn3(b_pair, pair(es.at[2], full, lane)))
        in_b = fac[1, :, lane] * (inner[3, :, lane] + nn3(b_pair, pair(es.at[3], full, lane)))
        gx_ref[:, lane] = in_f + in_b
        x = x_ref[:, lane]
        add_heads(tile, ((0, x * in_f), (1, x * in_b)))
        return carry

    def finish_outputs(tile, carry):
        lane = lanes(tile)
        full = slice(None)
        c_pair = (cs[0], cs[1])
        out_f = fac[2, :, lane] * (inner[0, :, lane] + nn3(c_pair, pair(es.at[0], full, lane)))
        out_b = fac[3, :, lane] * (inner[1, :, lane] + nn3(c_pair, pair(es.at[1], full, lane)))
        g = g_ref[:, lane]
        add_heads(tile, ((2, g * out_f), (3, g * out_b)))
        return carry

    def masked(m, source, tile, slot):
        lower = m in (0, 3)
        for r in range(2):
            row = slice(r * half, (r + 1) * half)
            depth = slice(0, (r + 1) * half) if lower else slice(r * half, length)
            left = (gm[m, 0, row, depth], gm[m, 1, row, depth])
            right = (xg[source, 0, depth, lanes(tile)], xg[source, 1, depth, lanes(tile)])
            inner[slot, row, lanes(tile)] = nn3(left, right)

    def input_side(tile, carry):
        masked(2, 2, tile, 2)
        masked(3, 3, tile, 3)
        return carry

    def output_side(tile, carry):
        masked(0, 0, tile, 0)
        masked(1, 1, tile, 1)
        return carry

    def square_side(tile, carry):
        low = iota((half, half), 0) >= iota((half, half), 1)
        high = iota((half, half), 0) <= iota((half, half), 1)
        upper = slice(0, half)
        under = slice(half, length)

        def block(a, row, b, col):
            return nt3(pair(xg.at[a], row, lanes(tile)), pair(xg.at[b], col, lanes(tile)))

        for part in (upper, under):
            amat[part, part] += jnp.where(low, block(2, part, 0, part), 0.0) + jnp.where(high, block(3, part, 1, part), 0.0)
        amat[under, upper] += block(2, under, 0, upper)
        amat[upper, under] += block(3, upper, 1, under)
        return carry

    loads[2].wait()
    turn(c_ref, cs, ct)
    loads[3].wait()
    for j in range(2):
        summarise(0, 2 * other + j, other, j * TILE)
    pl.semaphore_wait(barrier, CHIPS + 2)
    copies = to_partner(0)
    for j in range(2):
        summarise(0, 2 * core + j, core, j * TILE)
    for copy in copies:
        copy.wait()
    out_0 = gather(0)

    loads[4].wait()
    turn(b_ref, bs, bt)
    loads[5].wait()
    for j in range(2):
        summarise(1, 2 * other + j, other, j * TILE)
    copies = to_partner(1)
    for j in range(2):
        summarise(1, 2 * core + j, core, j * TILE)
    for copy in copies:
        copy.wait()
    out_1 = gather(1)

    for r in range(2):
        row = slice(r * half, (r + 1) * half)
        forward = nt3((cs[0, row], cs[1, row]), (bs[0], bs[1]))
        backward = nt3((bs[0, row], bs[1, row]), (cs[0], cs[1]))
        i = iota((half, length), 0) + r * half
        j = iota((half, length), 1)
        for m, (value, keep) in enumerate(((forward, i >= j), (forward, i <= j), (backward, i <= j), (backward, i >= j))):
            gm[m, 0, row], gm[m, 1, row] = split2(jnp.where(keep, value, 0.0))
    lax.fori_loop(0, 4, input_side, 0)

    back_0 = scan_chips(0, out_0)
    amat[...] = jnp.zeros_like(amat)
    red[...] = jnp.zeros_like(red)
    edge[...] = jnp.zeros_like(edge)
    lax.fori_loop(0, 4, square_side, 0)

    back_1 = scan_chips(1, out_1)
    whole_a = amat[...]
    from_b = nn3(split2(whole_a), (bs[0], bs[1]))
    from_c = nn3(split2(jnp.transpose(whole_a)), (cs[0], cs[1]))
    for r in range(2):
        acc[0, r] = from_c[r * half : (r + 1) * half]
        acc[1, r] = from_b[r * half : (r + 1) * half]
    lax.fori_loop(0, 4, output_side, 0)

    give = arrive(0, back_0)
    for j in range(2):
        project(0, core, j * TILE)
    give.wait()
    for j in range(2):
        project(0, other, j * TILE)
    zed_0 = exchange(0, 0, acc, z1, (z_even, z_odd))
    lax.fori_loop(0, 4, finish_inputs, 0)
    store = pltpu.make_async_copy(gx_ref, gx_hbm, store_sem.at[0])
    store.start()
    zed_0 = exchange_again(0, zed_0)

    give = arrive(1, back_1)
    for j in range(2):
        project(1, core, j * TILE)
    give.wait()
    for j in range(2):
        project(1, other, j * TILE)
    zed_1 = exchange(1, 0, acc, z1, (z_even, z_odd))
    exchange_end(0, zed_0, gb_ref)
    lax.fori_loop(0, 3, finish_outputs, 0)
    zed_1 = exchange_again(1, zed_1)
    lax.fori_loop(3, 4, finish_outputs, 0)

    sums = jnp.transpose(red[...])
    in_f, in_b, out_f, out_b = [sums[16 * m : 16 * m + heads] for m in range(4)]
    hot = (iota((4 * TILE, STATE), 1) == iota((4 * TILE, STATE), 0) // HEAD_DIM).astype(F32).astype(BF16)
    edges = [nn(p, hot) for p in split3(edge[...])]
    edges = jnp.transpose(edges[0] + (edges[1] + edges[2]))
    after = (rows >= cols).astype(F32).astype(BF16)

    def running(value, matrix):
        out = nn(jnp.concatenate(split3(value), axis=0), matrix)
        return out[:heads] + (out[heads : 2 * heads] + out[2 * heads :])

    log_grad = running(out_f - in_f, after) + edges[:heads, 0:1]
    log_grad = log_grad + running(out_b - in_b, upto) + edges[:heads, 1:2]
    graw_ref[...] = ((in_f + in_b) / step - rate * log_grad) * jax.nn.sigmoid(raw)

    exchange_end(1, zed_1, gc_ref)
    store.wait()


def hand_over(*refs):
    sources, targets, buffers, load_sem, store_sem = refs[:4], refs[4:8], refs[8:12], refs[12], refs[13]
    pieces = []
    for n in range(4):
        parts = 4 if n == 0 else 1
        rows = sources[n].shape[0] // parts
        pieces += [(n, pl.ds(p * rows, rows)) for p in range(parts)]
    loads = []
    for i, (n, row) in enumerate(pieces):
        loads.append(pltpu.make_async_copy(sources[n].at[row], buffers[n].at[row], load_sem.at[i]))
        loads[-1].start()
    stores = []
    for i, (n, row) in enumerate(pieces):
        loads[i].wait()
        stores.append(pltpu.make_async_copy(buffers[n].at[row], targets[n].at[row], store_sem.at[i]))
        stores[-1].start()
    for copy in stores:
        copy.wait()


def on_device(inputs, step_raw, decay_rate, b_proj, c_proj, grad_out):
    length, width = inputs.shape
    heads = step_raw.shape[0]
    vmem = pl.BlockSpec(memory_space=pltpu.VMEM)
    anywhere = pl.BlockSpec(memory_space=pl.ANY)
    block = (CHIPS, 2, 8, width // 2)
    square = (length, length)
    half = length // 2
    dma = pltpu.SemaphoreType.DMA
    scratch = [
        pltpu.VMEM((length, width), F32),
        pltpu.VMEM((length, width), F32),
        pltpu.VMEM((heads, length), F32),
        pltpu.VMEM((1, heads), F32),
        pltpu.VMEM((length, STATE), F32),
        pltpu.VMEM((length, STATE), F32),
        pltpu.VMEM((length, width), F32),
        pltpu.VMEM((length, 256), BF16),
        pltpu.VMEM((4, length, width), F32),
        pltpu.VMEM((4, 2, length, width), BF16),
        pltpu.VMEM((2, STATE, length), BF16),
        pltpu.VMEM((2, STATE, length), BF16),
        pltpu.VMEM((2, length, STATE), BF16),
        pltpu.VMEM((2, length, STATE), BF16),
        pltpu.VMEM((4, 2) + square, BF16),
        pltpu.VMEM(square, F32),
        pltpu.VMEM((4, length, width), F32),
        pltpu.VMEM((2, 2) + block, F32),
        pltpu.VMEM((2, 1, width // 2), F32),
        pltpu.VMEM((2,) + block, F32),
        pltpu.VMEM((1, width // 2), F32),
        pltpu.VMEM((2,) + block, F32),
        pltpu.VMEM((1, 1, width // 2), F32),
        pltpu.VMEM((2,) + block, F32),
        pltpu.VMEM((CHIPS, 1, width // 2), F32),
        pltpu.VMEM((2,) + block, F32),
        pltpu.VMEM((2,) + block, F32),
        pltpu.VMEM((2, 2) + block, F32),
        pltpu.VMEM((2,) + block, F32),
        pltpu.VMEM((4, 2, STATE, width), BF16),
        pltpu.VMEM((8, width), F32),
        pltpu.VMEM((2, 2, half, STATE), F32),
        pltpu.VMEM((2, 2, half, STATE), F32),
        pltpu.VMEM((2, 2, half, STATE), F32),
        pltpu.VMEM((2, 2, half, STATE), F32),
        pltpu.VMEM((length, STATE), F32),
        dma((6,)),
        dma((1,)),
        dma((3,)),
        dma((3,)),
        dma((2 * CHIPS,)),
        dma((2 * CHIPS,)),
        dma((CHIPS,)),
        dma((CHIPS,)),
        dma((2 * CHIPS,)),
        dma((2 * CHIPS,)),
        dma((2,)),
        dma((2,)),
        dma((8,)),
        dma((8,)),
    ]
    shapes = ((length, width), (heads, length), (length, STATE), (length, STATE))
    out_shape = tuple(jax.ShapeDtypeStruct(shape, F32) for shape in shapes)
    results = pl.pallas_call(
        kernel,
        out_shape=out_shape,
        in_specs=[anywhere] * 6,
        out_specs=(anywhere, vmem, vmem, vmem),
        scratch_shapes=scratch,
        compiler_params=pltpu.CompilerParams(
            collective_id=0, has_side_effects=True, vmem_limit_bytes=67043328
        ),
        name="scan_backward",
    )(inputs, grad_out, step_raw, decay_rate.reshape(1, heads), b_proj, c_proj)
    return pl.pallas_call(
        hand_over,
        out_shape=out_shape,
        in_specs=[anywhere] * 4,
        out_specs=(anywhere,) * 4,
        scratch_shapes=[pltpu.VMEM(shape, F32) for shape in shapes] + [dma((7,)), dma((7,))],
        name="hand_over",
    )(*results)


def solution(mesh):
    return jax.shard_map(
        on_device,
        mesh=mesh,
        in_specs=(
            P("seq", "head"),
            P("head", "seq"),
            P("head"),
            P("seq", None),
            P("seq", None),
            P("seq", "head"),
        ),
        out_specs=(P("seq", "head"), P("head", "seq"), P("seq", None), P("seq", None)),
        check_vma=False,
    )
```

```python
import jax
import jax.numpy as jnp
from jax import lax
from jax.experimental import pallas as pl
from jax.experimental.pallas import tpu as pltpu
from jax.sharding import PartitionSpec as P

HEAD_DIM = 64
STATE = 128
CHIPS = 16
TILE = 256
F32 = jnp.float32
BF16 = jnp.bfloat16
MESH = pl.DeviceIdType.MESH


def split2(a):
    high = a.astype(BF16)
    return high, (a - high.astype(F32)).astype(BF16)


def split3(a):
    first = a.astype(BF16)
    rest = a - first.astype(F32)
    second = rest.astype(BF16)
    return first, second, (rest - second.astype(F32)).astype(BF16)


def nn(a, b):
    return lax.dot_general(a, b, (((1,), (0,)), ((), ())), preferred_element_type=F32)


def nt(a, b):
    return lax.dot_general(a, b, (((1,), (1,)), ((), ())), preferred_element_type=F32)


def nn3(a, b):
    return nn(a[0], b[0]) + (nn(a[0], b[1]) + nn(a[1], b[0]))


def nt3(a, b):
    return nt(a[0], b[0]) + (nt(a[0], b[1]) + nt(a[1], b[0]))


def iota(shape, axis):
    return lax.broadcasted_iota(jnp.int32, shape, axis)


SOON = 15
OFFSETS = sorted(
    ((dx, dy) for dx in range(4) for dy in range(4) if dx or dy),
    key=lambda o: -(min(o[0], 4 - o[0]) + min(o[1], 4 - o[1])),
)


def kernel(
    x_hbm, g_hbm, raw_hbm, rate_hbm, b_hbm, c_hbm,
    gx_hbm, graw_ref, gb_ref, gc_ref,
    x_ref, g_ref, raw_ref, rate_ref, b_ref, c_ref, gx_ref,
    ft, fac, xg, bt, ct, bs, cs, gm, amat, inner,
    v, dec, pv, pdec, vc, dc, r1, dr, r2, r3, ein, eout, es, edge,
    acc, z1, acc2, z2, red,
    load_sem, store_sem, pair_send, pair_recv, out_send, out_recv, dec_send, dec_recv,
    back_send, back_recv, give_send, give_recv, z_send, z_recv,
):
    seq = lax.axis_index("seq")
    zed = lax.axis_index("head")
    chip = seq // 2
    core = seq % 2
    other = 1 - core
    chip_x = chip // 4
    chip_y = chip % 4
    partner = (2 * chip + other, zed)
    z_even = zed + 1 - 2 * (zed % 2)
    z_odd = (zed + 1 + 2 * ((zed + 1) % 2)) % 4
    length = x_ref.shape[0]
    heads = raw_ref.shape[0]
    half = length // 2
    quarter = half // 2
    first = (core == 0).astype(F32)
    second = 1.0 - first

    def peer(offset):
        dx, dy = OFFSETS[offset]
        return ((chip_x + dx) % 4) * 4 + (chip_y + dy) % 4

    def remote(src, dst, send, recv, device):
        return pltpu.make_async_remote_copy(src, dst, send, recv, device_id=device, device_id_type=MESH)

    barrier = pltpu.get_barrier_semaphore()
    for offset in range(CHIPS - 1):
        pl.semaphore_signal(barrier, inc=1, device_id=(2 * peer(offset) + core, zed), device_id_type=MESH)
    for target in (partner, (seq, z_even), (seq, z_odd)):
        pl.semaphore_signal(barrier, inc=1, device_id=target, device_id_type=MESH)
    loads = []
    for n, (src, dst) in enumerate((
        (raw_hbm, raw_ref), (rate_hbm, rate_ref), (c_hbm, c_ref), (g_hbm, g_ref), (b_hbm, b_ref), (x_hbm, x_ref)
    )):
        loads.append(pltpu.make_async_copy(src, dst, load_sem.at[n]))
        loads[-1].start()

    def lanes(tile):
        return pl.ds(pl.multiple_of(tile * TILE, TILE), TILE)

    rows = iota((length, length), 0)
    cols = iota((length, length), 1)
    upto = (rows <= cols).astype(F32).astype(BF16)
    loads[0].wait()
    loads[1].wait()
    raw = raw_ref[...]
    step = jnp.maximum(raw, 0.0) + jnp.log1p(jnp.exp(-jnp.abs(raw)))
    eye = iota((heads, heads), 0) == iota((heads, heads), 1)
    rate = jnp.sum(jnp.where(eye, rate_ref[...], 0.0), axis=1, keepdims=True)
    log_decay = -rate * step
    sums = nn(jnp.concatenate(split3(log_decay), axis=0), upto)
    run = sums[:heads] + (sums[heads : 2 * heads] + sums[2 * heads :])
    before = run - log_decay
    factors = jnp.concatenate(
        [step * jnp.exp(-run), step * jnp.exp(before), jnp.exp(run), jnp.exp(-before)], axis=0
    )
    parts = [p.astype(F32) for p in split3(factors)]
    stack = jnp.concatenate(parts + [jnp.zeros_like(factors)], axis=0)
    ft[...] = jnp.transpose(stack).astype(BF16)

    def turn(src, flat, turned):
        full = src[...]
        high, low = split2(full)
        flat[:, :STATE] = high
        flat[:, STATE : 2 * STATE] = high
        flat[:, 2 * STATE :] = low
        turned[0], turned[1] = split2(jnp.transpose(full))

    def halves(flat, row=slice(None)):
        return flat[row, :STATE], flat[row, 2 * STATE :]

    def pair(ref, *index):
        return ref[(0,) + index], ref[(1,) + index]

    def summarise(batch, tile, block, offset):
        spread = ft[...]
        r = iota((TILE, TILE), 0)
        col = iota((TILE, TILE), 1)
        source = (g_ref if batch == 0 else x_ref)[:, lanes(tile)]
        left = ct if batch == 0 else bt
        lane = slice(offset, offset + TILE)
        for q in ((2, 3) if batch == 0 else (1, 0)):
            hot = ((r % 64) == q * 16 + tile * 4 + col // HEAD_DIM) & (r < 192)
            factor = nn(spread, hot.astype(F32).astype(BF16))
            fac[q, :, lanes(tile)] = factor
            scaled = split2(factor * source)
            xg[q, 0, :, lanes(tile)] = scaled[0]
            xg[q, 1, :, lanes(tile)] = scaled[1]
            value = nn3((left[0], left[1]), scaled)
            if q == 2:
                dec[block, :, lane] = factor[length - 1 : length, :]
            if q in (0, 3):
                value = value * dec[block, :, lane]
            v[batch, block, :, int(q in (0, 3)), :, lane] = value.reshape(CHIPS, 8, TILE)

    def to_partner(batch):
        copies = [remote(v.at[batch, other], pv.at[batch], pair_send.at[batch], pair_recv.at[batch], partner)]
        if batch == 0:
            copies.append(remote(dec.at[other], pdec, pair_send.at[2], pair_recv.at[2], partner))
        for copy in copies:
            copy.start()
        return copies

    def gather(batch, offsets=range(CHIPS - 1)):
        own_decay = dec[core]
        mate_decay = pdec[...]
        if batch == 0:
            dc[0] = own_decay * mate_decay
        weights = (
            (first + second * mate_decay, first * own_decay + second),
            (first * mate_decay + second, first + second * own_decay),
        )

        def join(index):
            for flow in range(2):
                a, b = weights[flow]
                vc[batch, index, flow] = a * v[batch, core, index, flow] + b * pv[batch, index, flow]

        copies = []
        for offset in offsets:
            there = peer(offset)
            join(there)
            device = (2 * there + core, zed)
            n = batch * CHIPS + offset
            copies.append(remote(vc.at[batch, there], r1.at[batch, chip], out_send.at[n], out_recv.at[n], device))
            copies[-1].start()
            if batch == 0:
                copies.append(remote(dc.at[0], dr.at[chip], dec_send.at[offset], dec_recv.at[offset], device))
                copies[-1].start()
        if CHIPS - 2 in offsets:
            join(chip)
            r1[batch, chip] = vc[batch, chip]
        if batch == 0:
            dr[chip] = dc[0]
        return copies

    def scan_chips(batch, arrived):
        for copy in arrived:
            copy.wait_recv()
        state = jnp.zeros((8, 2 * TILE), F32)
        for index in range(CHIPS):
            r2[batch, index, 1] = state
            state = r1[batch, index, 1] + dr[index] * state
        state = jnp.zeros((8, 2 * TILE), F32)
        for index in reversed(range(CHIPS)):
            r2[batch, index, 0] = state
            state = r1[batch, index, 0] + dr[index] * state
        copies = []
        for offset in range(CHIPS - 1):
            there = peer(offset)
            n = batch * CHIPS + offset
            copies.append(remote(r2.at[batch, there], r3.at[batch, chip], back_send.at[n], back_recv.at[n], (2 * there + core, zed)))
            copies[-1].start()
        r3[batch, chip] = r2[batch, chip]
        return copies

    def arrive(batch, returned):
        own_decay = dec[core]
        mate_decay = pdec[...]
        gives = []
        for offset in range(-1, CHIPS - 1):
            index = chip
            if offset >= 0:
                dx, dy = OFFSETS[offset]
                index = ((chip_x + 4 - dx) % 4) * 4 + (chip_y + 4 - dy) % 4
                returned[offset].wait_recv()
            for flow in range(2):
                mine, mate = (second, first) if flow == 0 else (first, second)
                value = r3[batch, index, flow]
                ein[batch, core, index, flow] = (mine + mate * mate_decay) * value + mate * pv[batch, index, flow]
                eout[batch, index, flow] = (mate + mine * own_decay) * value + mine * v[batch, core, index, flow]
            n = batch * CHIPS + offset + 1
            gives.append(remote(eout.at[batch, index], ein.at[batch, core, index], give_send.at[n], give_recv.at[n], partner))
            gives[-1].start()
        return gives

    def project(batch, block, offset):
        tile = 2 * block + offset // TILE
        lane = slice(offset, offset + TILE)
        whole = dec[block, :, lane]
        early, late = [ein[batch, block, :, flow, :, lane].reshape(STATE, TILE) for flow in range(2)]
        if batch == 0:
            scaled = ((2, split2(whole * early)), (3, split2(late)))
        else:
            scaled = ((0, split2(late)), (1, split2(whole * early)))
            adjoint_early, adjoint_late = [ein[0, block, :, flow, :, lane].reshape(STATE, TILE) for flow in range(2)]
            local_early, local_late = [v[1, block, :, flow, :, lane].reshape(STATE, TILE) for flow in range(2)]
            edge[0:1, lanes(tile)] = jnp.sum(adjoint_early * (local_late + whole * late), axis=0, keepdims=True)
            edge[1:2, lanes(tile)] = jnp.sum(adjoint_late * (local_early + whole * early), axis=0, keepdims=True)
        total = None
        for m, value in scaled:
            es[m, :STATE, lanes(tile)] = value[0]
            es[m, STATE : 2 * STATE, lanes(tile)] = value[1]
            es[m, 2 * STATE :, lanes(tile)] = value[0]
            high, low = pair(xg.at[(m + 2) % 4], slice(None), lanes(tile))
            wide = nt(high, jnp.concatenate(value, axis=0))
            term = wide[:, :STATE] + (wide[:, STATE:] + nt(low, value[0]))
            total = term if total is None else total + term
        acc[batch] += total.reshape(2, 2, quarter, STATE)

    def exchange_part(batch, step_index, src, dst, part, r, targets):
        n = 8 * batch + 4 * step_index + 2 * part + r
        copy = remote(src.at[batch, r, part], dst.at[batch, r, part], z_send.at[n], z_recv.at[n], (seq, targets[r]))
        copy.start()
        return copy

    def exchange(batch):
        return [exchange_part(batch, 0, acc, z1, part, r, (z_even, z_odd)) for part in range(2) for r in range(2)]

    def exchange_again(batch, copies):
        onward = []
        for part in range(2):
            for r in range(2):
                copies[2 * part + r].wait()
                acc2[batch, r, part] = acc[batch, r, part] + z1[batch, r, part]
                onward.append(exchange_part(batch, 1, acc2, z2, part, r, (z_odd, z_even)))
        return onward

    def exchange_end(batch, copies, out):
        for part in range(2):
            for r in range(2):
                copies[2 * part + r].wait()
                start = r * half + part * quarter
                out[start : start + quarter] = acc2[batch, r, part] + z2[batch, r, part]

    def add_heads(tile, terms):
        r = iota((TILE, STATE), 0)
        col = iota((TILE, STATE), 1)
        total = red[...]
        for m, term in terms:
            hot = (col == 16 * m + tile * 4 + r // HEAD_DIM).astype(F32).astype(BF16)
            a, b = split2(term)
            total = total + (nn(a, hot) + nn(b, hot))
        red[...] = total

    def finish_inputs(tile, carry):
        lane = lanes(tile)
        in_f = fac[0, :, lane] * (inner[2, :, lane] + nn(bs[...], es[2, :, lane]))
        in_b = fac[1, :, lane] * (inner[3, :, lane] + nn(bs[...], es[3, :, lane]))
        gx_ref[:, lane] = in_f + in_b
        x = x_ref[:, lane]
        add_heads(tile, ((0, x * in_f), (1, x * in_b)))
        return carry

    def finish_outputs(tile, carry):
        lane = lanes(tile)
        out_f = fac[2, :, lane] * (inner[0, :, lane] + nn(cs[...], es[0, :, lane]))
        out_b = fac[3, :, lane] * (inner[1, :, lane] + nn(cs[...], es[1, :, lane]))
        g = g_ref[:, lane]
        add_heads(tile, ((2, g * out_f), (3, g * out_b)))
        return carry

    def masked(m, source, tile, slot):
        lower = m in (0, 3)
        for r in range(2):
            row = slice(r * half, (r + 1) * half)
            depth = slice(0, (r + 1) * half) if lower else slice(r * half, length)
            left = (gm[m, 0, row, depth], gm[m, 1, row, depth])
            right = (xg[source, 0, depth, lanes(tile)], xg[source, 1, depth, lanes(tile)])
            inner[slot, row, lanes(tile)] = nn3(left, right)

    def input_side(tile, carry):
        masked(2, 2, tile, 2)
        masked(3, 3, tile, 3)
        return carry

    def output_side(tile, carry):
        masked(0, 0, tile, 0)
        masked(1, 1, tile, 1)
        return carry

    def square_side(tile, carry):
        low = iota((half, half), 0) >= iota((half, half), 1)
        high = iota((half, half), 0) <= iota((half, half), 1)
        upper = slice(0, half)
        under = slice(half, length)

        def block(a, row, b, col):
            return nt3(pair(xg.at[a], row, lanes(tile)), pair(xg.at[b], col, lanes(tile)))

        for part in (upper, under):
            amat[part, part] += jnp.where(low, block(2, part, 0, part), 0.0) + jnp.where(high, block(3, part, 1, part), 0.0)
        amat[under, upper] += block(2, under, 0, upper)
        amat[upper, under] += block(3, upper, 1, under)
        return carry

    loads[2].wait()
    turn(c_ref, cs, ct)
    loads[3].wait()
    for j in range(2):
        summarise(0, 2 * other + j, other, j * TILE)
    for j in range(2):
        summarise(0, 2 * core + j, core, j * TILE)
    loads[4].wait()
    turn(b_ref, bs, bt)
    loads[5].wait()
    for j in range(2):
        summarise(1, 2 * other + j, other, j * TILE)
    for j in range(2):
        summarise(1, 2 * core + j, core, j * TILE)

    pl.semaphore_wait(barrier, CHIPS + 2)
    pair_0 = to_partner(0)
    pair_1 = to_partner(1)
    amat[...] = jnp.zeros_like(amat)
    red[...] = jnp.zeros_like(red)
    edge[...] = jnp.zeros_like(edge)
    for copy in pair_0:
        copy.wait()
    out_0 = gather(0)
    for copy in pair_1:
        copy.wait()
    out_1 = gather(1)

    for r in range(2):
        row = slice(r * half, (r + 1) * half)
        forward = nt3(halves(cs, row), halves(bs))
        backward = nt3(halves(bs, row), halves(cs))
        i = iota((half, length), 0) + r * half
        j = iota((half, length), 1)
        for m, (value, keep) in enumerate(((forward, i >= j), (forward, i <= j), (backward, i <= j), (backward, i >= j))):
            gm[m, 0, row], gm[m, 1, row] = split2(jnp.where(keep, value, 0.0))
    lax.fori_loop(0, 4, input_side, 0)

    lax.fori_loop(0, 4, square_side, 0)
    back_0 = scan_chips(0, out_0)
    for copy in out_0:
        copy.wait_send()

    whole_a = amat[...]
    from_b = nn3(split2(whole_a), halves(bs))
    from_c = nn3(split2(jnp.transpose(whole_a)), halves(cs))
    acc[0] = from_c.reshape(2, 2, quarter, STATE)
    acc[1] = from_b.reshape(2, 2, quarter, STATE)
    lax.fori_loop(0, 4, output_side, 0)

    for copy in back_0:
        copy.wait_send()
    for copy in out_1:
        copy.wait_send()
    back_1 = scan_chips(1, out_1)
    gives = arrive(0, back_0)
    for j in range(2):
        project(0, core, j * TILE)
    for give in gives:
        give.wait()
    for j in range(2):
        project(0, other, j * TILE)
    zed_0 = exchange(0)
    lax.fori_loop(0, 2, finish_inputs, 0)
    zed_0 = exchange_again(0, zed_0)

    for copy in back_1:
        copy.wait_send()
    gives = arrive(1, back_1)
    for j in range(2):
        project(1, core, j * TILE)
    for give in gives:
        give.wait()
    for j in range(2):
        project(1, other, j * TILE)
    zed_1 = exchange(1)
    lax.fori_loop(2, 4, finish_inputs, 0)
    store = pltpu.make_async_copy(gx_ref, gx_hbm, store_sem.at[0])
    store.start()
    exchange_end(0, zed_0, gb_ref)
    lax.fori_loop(0, 2, finish_outputs, 0)
    zed_1 = exchange_again(1, zed_1)
    lax.fori_loop(2, 4, finish_outputs, 0)

    sums = jnp.transpose(red[...])
    in_f, in_b, out_f, out_b = [sums[16 * m : 16 * m + heads] for m in range(4)]
    hot = (iota((4 * TILE, STATE), 1) == iota((4 * TILE, STATE), 0) // HEAD_DIM).astype(F32).astype(BF16)
    edges = [nn(p, hot) for p in split3(edge[...])]
    edges = jnp.transpose(edges[0] + (edges[1] + edges[2]))
    after = (rows >= cols).astype(F32).astype(BF16)

    def running(value, matrix):
        out = nn(jnp.concatenate(split3(value), axis=0), matrix)
        return out[:heads] + (out[heads : 2 * heads] + out[2 * heads :])

    log_grad = running(out_f - in_f, after) + edges[:heads, 0:1]
    log_grad = log_grad + running(out_b - in_b, upto) + edges[:heads, 1:2]
    graw_ref[...] = ((in_f + in_b) / step - rate * log_grad) * jax.nn.sigmoid(raw)

    exchange_end(1, zed_1, gc_ref)
    store.wait()


def hand_over(*refs):
    sources, targets, buffers, load_sem, store_sem = refs[:4], refs[4:8], refs[8:12], refs[12], refs[13]
    pieces = []
    for n in range(4):
        parts = 8 if n == 0 else 1
        rows = sources[n].shape[0] // parts
        pieces += [(n, pl.ds(p * rows, rows)) for p in range(parts)]
    loads = []
    for i, (n, row) in enumerate(pieces):
        loads.append(pltpu.make_async_copy(sources[n].at[row], buffers[n].at[row], load_sem.at[i]))
        loads[-1].start()
    stores = []
    for i, (n, row) in enumerate(pieces):
        loads[i].wait()
        stores.append(pltpu.make_async_copy(buffers[n].at[row], targets[n].at[row], store_sem.at[i]))
        stores[-1].start()
    for copy in stores:
        copy.wait()


def on_device(inputs, step_raw, decay_rate, b_proj, c_proj, grad_out):
    length, width = inputs.shape
    heads = step_raw.shape[0]
    vmem = pl.BlockSpec(memory_space=pltpu.VMEM)
    anywhere = pl.BlockSpec(memory_space=pl.ANY)
    block = (CHIPS, 2, 8, width // 2)
    square = (length, length)
    half = length // 2
    dma = pltpu.SemaphoreType.DMA
    scratch = [
        pltpu.VMEM((length, width), F32),
        pltpu.VMEM((length, width), F32),
        pltpu.VMEM((heads, length), F32),
        pltpu.VMEM((1, heads), F32),
        pltpu.VMEM((length, STATE), F32),
        pltpu.VMEM((length, STATE), F32),
        pltpu.VMEM((length, width), F32),
        pltpu.VMEM((length, 256), BF16),
        pltpu.VMEM((4, length, width), F32),
        pltpu.VMEM((4, 2, length, width), BF16),
        pltpu.VMEM((2, STATE, length), BF16),
        pltpu.VMEM((2, STATE, length), BF16),
        pltpu.VMEM((length, 3 * STATE), BF16),
        pltpu.VMEM((length, 3 * STATE), BF16),
        pltpu.VMEM((4, 2) + square, BF16),
        pltpu.VMEM(square, F32),
        pltpu.VMEM((4, length, width), F32),
        pltpu.VMEM((2, 2) + block, F32),
        pltpu.VMEM((2, 1, width // 2), F32),
        pltpu.VMEM((2,) + block, F32),
        pltpu.VMEM((1, width // 2), F32),
        pltpu.VMEM((2,) + block, F32),
        pltpu.VMEM((1, 1, width // 2), F32),
        pltpu.VMEM((2,) + block, F32),
        pltpu.VMEM((CHIPS, 1, width // 2), F32),
        pltpu.VMEM((2,) + block, F32),
        pltpu.VMEM((2,) + block, F32),
        pltpu.VMEM((2, 2) + block, F32),
        pltpu.VMEM((2,) + block, F32),
        pltpu.VMEM((4, 3 * STATE, width), BF16),
        pltpu.VMEM((8, width), F32),
        pltpu.VMEM((2, 2, 2, half // 2, STATE), F32),
        pltpu.VMEM((2, 2, 2, half // 2, STATE), F32),
        pltpu.VMEM((2, 2, 2, half // 2, STATE), F32),
        pltpu.VMEM((2, 2, 2, half // 2, STATE), F32),
        pltpu.VMEM((length, STATE), F32),
        dma((6,)),
        dma((1,)),
        dma((3,)),
        dma((3,)),
        dma((2 * CHIPS,)),
        dma((2 * CHIPS,)),
        dma((CHIPS,)),
        dma((CHIPS,)),
        dma((2 * CHIPS,)),
        dma((2 * CHIPS,)),
        dma((2 * CHIPS,)),
        dma((2 * CHIPS,)),
        dma((16,)),
        dma((16,)),
    ]
    shapes = ((length, width), (heads, length), (length, STATE), (length, STATE))
    out_shape = tuple(jax.ShapeDtypeStruct(shape, F32) for shape in shapes)
    results = pl.pallas_call(
        kernel,
        out_shape=out_shape,
        in_specs=[anywhere] * 6,
        out_specs=(anywhere, vmem, vmem, vmem),
        scratch_shapes=scratch,
        compiler_params=pltpu.CompilerParams(
            collective_id=0, has_side_effects=True, vmem_limit_bytes=67043328
        ),
        name="scan_backward",
    )(inputs, grad_out, step_raw, decay_rate.reshape(1, heads), b_proj, c_proj)
    return pl.pallas_call(
        hand_over,
        out_shape=out_shape,
        in_specs=[anywhere] * 4,
        out_specs=(anywhere,) * 4,
        scratch_shapes=[pltpu.VMEM(shape, F32) for shape in shapes] + [dma((11,)), dma((11,))],
        name="hand_over",
    )(*results)


def solution(mesh):
    return jax.shard_map(
        on_device,
        mesh=mesh,
        in_specs=(
            P("seq", "head"),
            P("head", "seq"),
            P("head"),
            P("seq", None),
            P("seq", None),
            P("seq", "head"),
        ),
        out_specs=(P("seq", "head"), P("head", "seq"), P("seq", None), P("seq", None)),
        check_vma=False,
    )
```

```python
import jax
import jax.numpy as jnp
from jax import lax
from jax.experimental import pallas as pl
from jax.experimental.pallas import tpu as pltpu
from jax.sharding import PartitionSpec as P

HEAD_DIM = 64
STATE = 128
CHIPS = 16
TILE = 256
F32 = jnp.float32
BF16 = jnp.bfloat16
MESH = pl.DeviceIdType.MESH


def split2(a):
    high = a.astype(BF16)
    return high, (a - high.astype(F32)).astype(BF16)


def split3(a):
    first = a.astype(BF16)
    rest = a - first.astype(F32)
    second = rest.astype(BF16)
    return first, second, (rest - second.astype(F32)).astype(BF16)


def nn(a, b):
    return lax.dot_general(a, b, (((1,), (0,)), ((), ())), preferred_element_type=F32)


def nt(a, b):
    return lax.dot_general(a, b, (((1,), (1,)), ((), ())), preferred_element_type=F32)


def nn3(a, b):
    return nn(a[0], b[0]) + (nn(a[0], b[1]) + nn(a[1], b[0]))


def nt3(a, b):
    return nt(a[0], b[0]) + (nt(a[0], b[1]) + nt(a[1], b[0]))


def iota(shape, axis):
    return lax.broadcasted_iota(jnp.int32, shape, axis)


OFFSETS = sorted(
    ((dx, dy) for dx in range(4) for dy in range(4) if dx or dy),
    key=lambda o: -(min(o[0], 4 - o[0]) + min(o[1], 4 - o[1])),
)


def kernel(
    x_hbm, g_hbm, raw_hbm, rate_hbm, b_hbm, c_hbm,
    gx_ref, graw_ref, gb_ref, gc_ref,
    x_ref, g_ref, raw_ref, rate_ref, b_ref, c_ref,
    ft, fac, xg, bt, ct, bs, cs, gm, amat, inner,
    v, dec, pv, pdec, vc, dc, r1, dr, r2, r3, ein, eout, es, edge,
    acc, z1, acc2, z2, red,
    load_sem, pair_send, pair_recv, out_send, out_recv, dec_send, dec_recv,
    back_send, back_recv, give_send, give_recv, z_send, z_recv,
):
    seq = lax.axis_index("seq")
    zed = lax.axis_index("head")
    chip = seq // 2
    core = seq % 2
    other = 1 - core
    chip_x = chip // 4
    chip_y = chip % 4
    partner = (2 * chip + other, zed)
    z_even = zed + 1 - 2 * (zed % 2)
    z_odd = (zed + 1 + 2 * ((zed + 1) % 2)) % 4
    length = x_ref.shape[0]
    heads = raw_ref.shape[0]
    half = length // 2
    quarter = half // 2
    first = (core == 0).astype(F32)
    second = 1.0 - first

    def peer(offset):
        dx, dy = OFFSETS[offset]
        return ((chip_x + dx) % 4) * 4 + (chip_y + dy) % 4

    def remote(src, dst, send, recv, device):
        return pltpu.make_async_remote_copy(src, dst, send, recv, device_id=device, device_id_type=MESH)

    barrier = pltpu.get_barrier_semaphore()
    for offset in range(CHIPS - 1):
        pl.semaphore_signal(barrier, inc=1, device_id=(2 * peer(offset) + core, zed), device_id_type=MESH)
    for target in (partner, (seq, z_even), (seq, z_odd)):
        pl.semaphore_signal(barrier, inc=1, device_id=target, device_id_type=MESH)
    loads = []
    for n, (src, dst) in enumerate((
        (raw_hbm, raw_ref), (rate_hbm, rate_ref), (c_hbm, c_ref), (g_hbm, g_ref), (b_hbm, b_ref), (x_hbm, x_ref)
    )):
        loads.append(pltpu.make_async_copy(src, dst, load_sem.at[n]))
        loads[-1].start()

    def lanes(tile):
        return pl.ds(pl.multiple_of(tile * TILE, TILE), TILE)

    rows = iota((length, length), 0)
    cols = iota((length, length), 1)
    upto = (rows <= cols).astype(F32).astype(BF16)
    loads[0].wait()
    loads[1].wait()
    raw = raw_ref[...]
    step = jnp.maximum(raw, 0.0) + jnp.log1p(jnp.exp(-jnp.abs(raw)))
    eye = iota((heads, heads), 0) == iota((heads, heads), 1)
    rate = jnp.sum(jnp.where(eye, rate_ref[...], 0.0), axis=1, keepdims=True)
    log_decay = -rate * step
    sums = nn(jnp.concatenate(split3(log_decay), axis=0), upto)
    run = sums[:heads] + (sums[heads : 2 * heads] + sums[2 * heads :])
    before = run - log_decay
    factors = jnp.concatenate(
        [step * jnp.exp(-run), step * jnp.exp(before), jnp.exp(run), jnp.exp(-before)], axis=0
    )
    parts = [p.astype(F32) for p in split3(factors)]
    stack = jnp.concatenate(parts + [jnp.zeros_like(factors)], axis=0)
    ft[...] = jnp.transpose(stack).astype(BF16)

    def turn(src, flat, turned):
        full = src[...]
        high, low = split2(full)
        flat[:, :STATE] = high
        flat[:, STATE : 2 * STATE] = high
        flat[:, 2 * STATE :] = low
        turned[0], turned[1] = split2(jnp.transpose(full))

    def halves(flat, row=slice(None)):
        return flat[row, :STATE], flat[row, 2 * STATE :]

    def pair(ref, *index):
        return ref[(0,) + index], ref[(1,) + index]

    def summarise(batch, tile, block, offset):
        spread = ft[...]
        r = iota((TILE, TILE), 0)
        col = iota((TILE, TILE), 1)
        source = (g_ref if batch == 0 else x_ref)[:, lanes(tile)]
        left = ct if batch == 0 else bt
        lane = slice(offset, offset + TILE)
        for q in ((2, 3) if batch == 0 else (1, 0)):
            hot = ((r % 64) == q * 16 + tile * 4 + col // HEAD_DIM) & (r < 192)
            factor = nn(spread, hot.astype(F32).astype(BF16))
            fac[q, :, lanes(tile)] = factor
            scaled = split2(factor * source)
            xg[q, 0, :, lanes(tile)] = scaled[0]
            xg[q, 1, :, lanes(tile)] = scaled[1]
            value = nn3((left[0], left[1]), scaled)
            if q == 2:
                dec[block, :, lane] = factor[length - 1 : length, :]
            if q in (0, 3):
                value = value * dec[block, :, lane]
            v[batch, block, :, int(q in (0, 3)), :, lane] = value.reshape(CHIPS, 8, TILE)

    def to_partner(batch):
        copies = [remote(v.at[batch, other], pv.at[batch], pair_send.at[batch], pair_recv.at[batch], partner)]
        if batch == 0:
            copies.append(remote(dec.at[other], pdec, pair_send.at[2], pair_recv.at[2], partner))
        for copy in copies:
            copy.start()
        return copies

    def gather(batch, offsets=range(CHIPS - 1)):
        own_decay = dec[core]
        mate_decay = pdec[...]
        if batch == 0:
            dc[0] = own_decay * mate_decay
        weights = (
            (first + second * mate_decay, first * own_decay + second),
            (first * mate_decay + second, first + second * own_decay),
        )

        def join(index):
            for flow in range(2):
                a, b = weights[flow]
                vc[batch, index, flow] = a * v[batch, core, index, flow] + b * pv[batch, index, flow]

        copies = []
        for offset in offsets:
            there = peer(offset)
            join(there)
            device = (2 * there + core, zed)
            n = batch * CHIPS + offset
            copies.append(remote(vc.at[batch, there], r1.at[batch, chip], out_send.at[n], out_recv.at[n], device))
            copies[-1].start()
            if batch == 0:
                copies.append(remote(dc.at[0], dr.at[chip], dec_send.at[offset], dec_recv.at[offset], device))
                copies[-1].start()
        if CHIPS - 2 in offsets:
            join(chip)
            r1[batch, chip] = vc[batch, chip]
        if batch == 0:
            dr[chip] = dc[0]
        return copies

    def scan_chips(batch, arrived):
        for copy in arrived:
            copy.wait_recv()
        state = jnp.zeros((8, 2 * TILE), F32)
        for index in range(CHIPS):
            r2[batch, index, 1] = state
            state = r1[batch, index, 1] + dr[index] * state
        state = jnp.zeros((8, 2 * TILE), F32)
        for index in reversed(range(CHIPS)):
            r2[batch, index, 0] = state
            state = r1[batch, index, 0] + dr[index] * state
        copies = []
        for offset in range(CHIPS - 1):
            there = peer(offset)
            n = batch * CHIPS + offset
            copies.append(remote(r2.at[batch, there], r3.at[batch, chip], back_send.at[n], back_recv.at[n], (2 * there + core, zed)))
            copies[-1].start()
        r3[batch, chip] = r2[batch, chip]
        return copies

    def arrive(batch, returned):
        own_decay = dec[core]
        mate_decay = pdec[...]
        gives = []
        for offset in range(-1, CHIPS - 1):
            index = chip
            if offset >= 0:
                dx, dy = OFFSETS[offset]
                index = ((chip_x + 4 - dx) % 4) * 4 + (chip_y + 4 - dy) % 4
                returned[offset].wait_recv()
            for flow in range(2):
                mine, mate = (second, first) if flow == 0 else (first, second)
                value = r3[batch, index, flow]
                ein[batch, core, index, flow] = (mine + mate * mate_decay) * value + mate * pv[batch, index, flow]
                eout[batch, index, flow] = (mate + mine * own_decay) * value + mine * v[batch, core, index, flow]
            n = batch * CHIPS + offset + 1
            gives.append(remote(eout.at[batch, index], ein.at[batch, core, index], give_send.at[n], give_recv.at[n], partner))
            gives[-1].start()
        return gives

    def project(batch, block, offset):
        tile = 2 * block + offset // TILE
        lane = slice(offset, offset + TILE)
        whole = dec[block, :, lane]
        early, late = [ein[batch, block, :, flow, :, lane].reshape(STATE, TILE) for flow in range(2)]
        if batch == 0:
            scaled = ((2, split2(whole * early)), (3, split2(late)))
        else:
            scaled = ((0, split2(late)), (1, split2(whole * early)))
            adjoint_early, adjoint_late = [ein[0, block, :, flow, :, lane].reshape(STATE, TILE) for flow in range(2)]
            local_early, local_late = [v[1, block, :, flow, :, lane].reshape(STATE, TILE) for flow in range(2)]
            edge[0:1, lanes(tile)] = jnp.sum(adjoint_early * (local_late + whole * late), axis=0, keepdims=True)
            edge[1:2, lanes(tile)] = jnp.sum(adjoint_late * (local_early + whole * early), axis=0, keepdims=True)
        total = None
        for m, value in scaled:
            es[m, :STATE, lanes(tile)] = value[0]
            es[m, STATE : 2 * STATE, lanes(tile)] = value[1]
            es[m, 2 * STATE :, lanes(tile)] = value[0]
            high, low = pair(xg.at[(m + 2) % 4], slice(None), lanes(tile))
            wide = nt(high, jnp.concatenate(value, axis=0))
            term = wide[:, :STATE] + (wide[:, STATE:] + nt(low, value[0]))
            total = term if total is None else total + term
        acc[batch] += total.reshape(2, 2, quarter, STATE)

    def exchange_part(batch, step_index, src, dst, part, r, targets):
        n = 8 * batch + 4 * step_index + 2 * part + r
        copy = remote(src.at[batch, r, part], dst.at[batch, r, part], z_send.at[n], z_recv.at[n], (seq, targets[r]))
        copy.start()
        return copy

    def exchange(batch):
        return [exchange_part(batch, 0, acc, z1, part, r, (z_even, z_odd)) for part in range(2) for r in range(2)]

    def exchange_again(batch, copies):
        onward = []
        for part in range(2):
            for r in range(2):
                copies[2 * part + r].wait()
                acc2[batch, r, part] = acc[batch, r, part] + z1[batch, r, part]
                onward.append(exchange_part(batch, 1, acc2, z2, part, r, (z_odd, z_even)))
        return onward

    def exchange_end(batch, copies, out):
        for part in range(2):
            for r in range(2):
                copies[2 * part + r].wait()
                start = r * half + part * quarter
                out[start : start + quarter] = acc2[batch, r, part] + z2[batch, r, part]

    def add_heads(tile, terms):
        r = iota((TILE, STATE), 0)
        col = iota((TILE, STATE), 1)
        total = red[...]
        for m, term in terms:
            hot = (col == 16 * m + tile * 4 + r // HEAD_DIM).astype(F32).astype(BF16)
            a, b = split2(term)
            total = total + (nn(a, hot) + nn(b, hot))
        red[...] = total

    def finish_inputs(tile, carry):
        lane = lanes(tile)
        in_f = fac[0, :, lane] * (inner[2, :, lane] + nn(bs[...], es[2, :, lane]))
        in_b = fac[1, :, lane] * (inner[3, :, lane] + nn(bs[...], es[3, :, lane]))
        gx_ref[:, lane] = in_f + in_b
        x = x_ref[:, lane]
        add_heads(tile, ((0, x * in_f), (1, x * in_b)))
        return carry

    def finish_outputs(tile, carry):
        lane = lanes(tile)
        out_f = fac[2, :, lane] * (inner[0, :, lane] + nn(cs[...], es[0, :, lane]))
        out_b = fac[3, :, lane] * (inner[1, :, lane] + nn(cs[...], es[1, :, lane]))
        g = g_ref[:, lane]
        add_heads(tile, ((2, g * out_f), (3, g * out_b)))
        return carry

    def masked(m, source, tile, slot):
        lower = m in (0, 3)
        for r in range(2):
            row = slice(r * half, (r + 1) * half)
            depth = slice(0, (r + 1) * half) if lower else slice(r * half, length)
            left = (gm[m, 0, row, depth], gm[m, 1, row, depth])
            right = (xg[source, 0, depth, lanes(tile)], xg[source, 1, depth, lanes(tile)])
            inner[slot, row, lanes(tile)] = nn3(left, right)

    def input_side(tile, carry):
        masked(2, 2, tile, 2)
        masked(3, 3, tile, 3)
        return carry

    def output_side(tile, carry):
        masked(0, 0, tile, 0)
        masked(1, 1, tile, 1)
        return carry

    def square_side(tile, carry):
        low = iota((half, half), 0) >= iota((half, half), 1)
        high = iota((half, half), 0) <= iota((half, half), 1)
        upper = slice(0, half)
        under = slice(half, length)

        def block(a, row, b, col):
            return nt3(pair(xg.at[a], row, lanes(tile)), pair(xg.at[b], col, lanes(tile)))

        for part in (upper, under):
            amat[part, part] += jnp.where(low, block(2, part, 0, part), 0.0) + jnp.where(high, block(3, part, 1, part), 0.0)
        amat[under, upper] += block(2, under, 0, upper)
        amat[upper, under] += block(3, upper, 1, under)
        return carry

    loads[2].wait()
    turn(c_ref, cs, ct)
    loads[3].wait()
    for j in range(2):
        summarise(0, 2 * other + j, other, j * TILE)
    for j in range(2):
        summarise(0, 2 * core + j, core, j * TILE)
    loads[4].wait()
    turn(b_ref, bs, bt)
    loads[5].wait()
    for j in range(2):
        summarise(1, 2 * other + j, other, j * TILE)
    for j in range(2):
        summarise(1, 2 * core + j, core, j * TILE)

    pl.semaphore_wait(barrier, CHIPS + 2)
    pair_0 = to_partner(0)
    pair_1 = to_partner(1)
    amat[...] = jnp.zeros_like(amat)
    red[...] = jnp.zeros_like(red)
    edge[...] = jnp.zeros_like(edge)
    for copy in pair_0:
        copy.wait()
    out_0 = gather(0)
    for copy in pair_1:
        copy.wait()
    out_1 = gather(1)

    for r in range(2):
        row = slice(r * half, (r + 1) * half)
        forward = nt3(halves(cs, row), halves(bs))
        backward = nt3(halves(bs, row), halves(cs))
        i = iota((half, length), 0) + r * half
        j = iota((half, length), 1)
        for m, (value, keep) in enumerate(((forward, i >= j), (forward, i <= j), (backward, i <= j), (backward, i >= j))):
            gm[m, 0, row], gm[m, 1, row] = split2(jnp.where(keep, value, 0.0))
    lax.fori_loop(0, 4, input_side, 0)

    lax.fori_loop(0, 4, square_side, 0)
    back_0 = scan_chips(0, out_0)
    for copy in out_0:
        copy.wait_send()

    whole_a = amat[...]
    from_b = nn3(split2(whole_a), halves(bs))
    from_c = nn3(split2(jnp.transpose(whole_a)), halves(cs))
    acc[0] = from_c.reshape(2, 2, quarter, STATE)
    acc[1] = from_b.reshape(2, 2, quarter, STATE)
    lax.fori_loop(0, 4, output_side, 0)

    for copy in back_0:
        copy.wait_send()
    for copy in out_1:
        copy.wait_send()
    back_1 = scan_chips(1, out_1)
    gives = arrive(0, back_0)
    for j in range(2):
        project(0, core, j * TILE)
    for give in gives:
        give.wait()
    for j in range(2):
        project(0, other, j * TILE)
    zed_0 = exchange(0)
    lax.fori_loop(0, 2, finish_inputs, 0)
    zed_0 = exchange_again(0, zed_0)

    for copy in back_1:
        copy.wait_send()
    gives = arrive(1, back_1)
    for j in range(2):
        project(1, core, j * TILE)
    for give in gives:
        give.wait()
    for j in range(2):
        project(1, other, j * TILE)
    zed_1 = exchange(1)
    lax.fori_loop(2, 4, finish_inputs, 0)
    exchange_end(0, zed_0, gb_ref)
    lax.fori_loop(0, 2, finish_outputs, 0)
    zed_1 = exchange_again(1, zed_1)
    lax.fori_loop(2, 4, finish_outputs, 0)

    sums = jnp.transpose(red[...])
    in_f, in_b, out_f, out_b = [sums[16 * m : 16 * m + heads] for m in range(4)]
    hot = (iota((4 * TILE, STATE), 1) == iota((4 * TILE, STATE), 0) // HEAD_DIM).astype(F32).astype(BF16)
    edges = [nn(p, hot) for p in split3(edge[...])]
    edges = jnp.transpose(edges[0] + (edges[1] + edges[2]))
    after = (rows >= cols).astype(F32).astype(BF16)

    def running(value, matrix):
        out = nn(jnp.concatenate(split3(value), axis=0), matrix)
        return out[:heads] + (out[heads : 2 * heads] + out[2 * heads :])

    log_grad = running(out_f - in_f, after) + edges[:heads, 0:1]
    log_grad = log_grad + running(out_b - in_b, upto) + edges[:heads, 1:2]
    graw_ref[...] = ((in_f + in_b) / step - rate * log_grad) * jax.nn.sigmoid(raw)

    exchange_end(1, zed_1, gc_ref)


def on_device(inputs, step_raw, decay_rate, b_proj, c_proj, grad_out):
    length, width = inputs.shape
    heads = step_raw.shape[0]
    vmem = pl.BlockSpec(memory_space=pltpu.VMEM)
    anywhere = pl.BlockSpec(memory_space=pl.ANY)
    block = (CHIPS, 2, 8, width // 2)
    square = (length, length)
    half = length // 2
    dma = pltpu.SemaphoreType.DMA
    scratch = [
        pltpu.VMEM((length, width), F32),
        pltpu.VMEM((length, width), F32),
        pltpu.VMEM((heads, length), F32),
        pltpu.VMEM((1, heads), F32),
        pltpu.VMEM((length, STATE), F32),
        pltpu.VMEM((length, STATE), F32),
        pltpu.VMEM((length, 256), BF16),
        pltpu.VMEM((4, length, width), F32),
        pltpu.VMEM((4, 2, length, width), BF16),
        pltpu.VMEM((2, STATE, length), BF16),
        pltpu.VMEM((2, STATE, length), BF16),
        pltpu.VMEM((length, 3 * STATE), BF16),
        pltpu.VMEM((length, 3 * STATE), BF16),
        pltpu.VMEM((4, 2) + square, BF16),
        pltpu.VMEM(square, F32),
        pltpu.VMEM((4, length, width), F32),
        pltpu.VMEM((2, 2) + block, F32),
        pltpu.VMEM((2, 1, width // 2), F32),
        pltpu.VMEM((2,) + block, F32),
        pltpu.VMEM((1, width // 2), F32),
        pltpu.VMEM((2,) + block, F32),
        pltpu.VMEM((1, 1, width // 2), F32),
        pltpu.VMEM((2,) + block, F32),
        pltpu.VMEM((CHIPS, 1, width // 2), F32),
        pltpu.VMEM((2,) + block, F32),
        pltpu.VMEM((2,) + block, F32),
        pltpu.VMEM((2, 2) + block, F32),
        pltpu.VMEM((2,) + block, F32),
        pltpu.VMEM((4, 3 * STATE, width), BF16),
        pltpu.VMEM((8, width), F32),
        pltpu.VMEM((2, 2, 2, half // 2, STATE), F32),
        pltpu.VMEM((2, 2, 2, half // 2, STATE), F32),
        pltpu.VMEM((2, 2, 2, half // 2, STATE), F32),
        pltpu.VMEM((2, 2, 2, half // 2, STATE), F32),
        pltpu.VMEM((length, STATE), F32),
        dma((6,)),
        dma((3,)),
        dma((3,)),
        dma((2 * CHIPS,)),
        dma((2 * CHIPS,)),
        dma((CHIPS,)),
        dma((CHIPS,)),
        dma((2 * CHIPS,)),
        dma((2 * CHIPS,)),
        dma((2 * CHIPS,)),
        dma((2 * CHIPS,)),
        dma((16,)),
        dma((16,)),
    ]
    shapes = ((length, width), (heads, length), (length, STATE), (length, STATE))
    results = pl.pallas_call(
        kernel,
        out_shape=tuple(pltpu.VMEM(shape, F32) for shape in shapes),
        in_specs=[anywhere] * 6,
        out_specs=(vmem,) * 4,
        scratch_shapes=scratch,
        compiler_params=pltpu.CompilerParams(
            collective_id=0, has_side_effects=True, vmem_limit_bytes=60 * 2**20
        ),
        name="scan_backward",
    )(inputs, grad_out, step_raw, decay_rate.reshape(1, heads), b_proj, c_proj)
    return results


def solution(mesh):
    return jax.shard_map(
        on_device,
        mesh=mesh,
        in_specs=(
            P("seq", "head"),
            P("head", "seq"),
            P("head"),
            P("seq", None),
            P("seq", None),
            P("seq", "head"),
        ),
        out_specs=(P("seq", "head"), P("head", "seq"), P("seq", None), P("seq", None)),
        check_vma=False,
    )
```
